32 devices in a mesh: dp: 8 (over z, x), ctx: 4 (over y, core).
Axes of the slice: x: 2, y: 2, z: 4, core: 2. Of those that a mesh axis runs over, the one named last changes fastest.
Arguments:
- tokens: bfloat16 [4096, 1024], P(('dp', 'ctx')), may hold values from -6 to 6
- cotangent: bfloat16 [4096, 1024], P(('dp', 'ctx')), may hold values from -6 to 6
- segment_ids: int32 [8, 512], P('dp'), may hold values from 0 to 3, never falling along the last dimension, each value on 1 to 256 neighbouring positions
- tract_order: int32 [8, 8], P('dp'), may hold values from 0 to 7, each once within a row
- qkv_weight: bfloat16 [1024, 3072], P(('dp', 'ctx')), may hold values from -0.1875 to 0.1875
- out_weight: bfloat16 [1024, 1024], P(('dp', 'ctx')), may hold values from -2 to 2
- up_weight: bfloat16 [1024, 4096], P(('dp', 'ctx')), may hold values from -0.1875 to 0.1875
- down_weight: bfloat16 [4096, 1024], P(('dp', 'ctx')), may hold values from -0.09375 to 0.09375
- norm_gain: bfloat16 [2, 1024], P(None, ('dp', 'ctx')), may hold values from 0.5 to 1.5
- norm_shift: bfloat16 [2, 1024], P(None, ('dp', 'ctx')), may hold values from -4 to 4
- proj_bias: bfloat16 [4, 1024], P(None, ('dp', 'ctx')), may hold values from -6 to 6
- up_bias: bfloat16 [4096], P(('dp', 'ctx')), may hold values from -6 to 6
Outputs:
- block_out: float32 [4096, 1024], P(('dp', 'ctx'))
- input_grad: float32 [4096, 1024], P(('dp', 'ctx'))
- qkv_weight_grad: float32 [1024, 3072], P(('dp', 'ctx'))
- out_weight_grad: float32 [1024, 1024], P(('dp', 'ctx'))
- up_weight_grad: float32 [1024, 4096], P(('dp', 'ctx'))
- down_weight_grad: float32 [4096, 1024], P(('dp', 'ctx'))
- norm_gain_grad: float32 [2, 1024], P(None, ('dp', 'ctx'))
- norm_shift_grad: float32 [2, 1024], P(None, ('dp', 'ctx'))
- proj_bias_grad: float32 [4, 1024], P(None, ('dp', 'ctx'))
- up_bias_grad: float32 [4096], P(('dp', 'ctx'))
The draws below stay inside these ranges and needn't reach their ends.
Inputs may be any that keep to these rules, and one draw needn't show every extreme that they name: `segment_ids`: along each row the ids never fall; one document covers at most 256 positions of a row. `tract_order`: each row is a permutation: every place 0 to 7 is named once.
All inputs are finite; a program needn't handle non-finite values.
Results may differ from the reference program's by a relative error of at most 0.011.
Values may be sent and summed in bfloat16 or wider, within the bound.
A program may use at most 256 MiB of HBM per device.

```python
import math
import jax
import jax.numpy as jnp
import numpy as np
from jax import lax

D = 1024
HEADS = 16
HEAD_DIM = 64
FF = 4096
STRETCH = 64
STRETCHES = 8
SEQ_LEN = 512
SEQS = 8
TOKENS = 4096


def levels(key, extent, split, low, high):
    level, own = 1.0, jax.random.fold_in(key, 6)
    for dim, parts in split:
        draws = jnp.exp(jax.random.uniform(jax.random.fold_in(own, dim), (parts,), jnp.float32, low / len(split), high / len(split)))
        level = level * jnp.repeat(draws, extent[dim] // parts).reshape([-1 if axis == dim else 1 for axis in range(len(extent))])
    return level


def split_up(number_of, total, most, skew):
    loads = [(1 << 20) // math.isqrt(standing ** skew) + 1 for standing in range(2, number_of + 1)]
    surplus, holding = total - most - (number_of - 1), [1] * (number_of - 1)
    while surplus > 0:
        candidates = [i for i in range(number_of - 1) if holding[i] < most]
        mass, remaining = sum([loads[i] for i in candidates]), surplus
        for i in candidates:
            more = min(most - holding[i], max(1, remaining * loads[i] // mass), surplus)
            holding[i] = holding[i] + more
            surplus = surplus - more
    return np.array([most] + holding)


def uneven(stream_key, count, total, reach, skew):
    if count == 2:
        one = jax.random.randint(stream_key, (), max(1, total - reach), min(reach, total - 1) + 1)
        return jnp.stack([one, total - one])
    tallies = jnp.asarray(split_up(count, total, reach, skew), jnp.int32)
    twos = (count - 1) // 2
    donor, receiver = tallies[1:1 + 2 * twos:2], tallies[2:2 + 2 * twos:2]
    slack = jnp.minimum(donor - 1, reach - receiver)
    passed = jax.random.randint(jax.random.fold_in(stream_key, 1), (twos,), 0, 1 << 20) % (slack + 1)
    tallies = tallies.at[1:1 + 2 * twos:2].set(donor - passed).at[2:2 + 2 * twos:2].set(receiver + passed)
    return tallies[jax.random.permutation(jax.random.fold_in(stream_key, 2), count)]


def normal_values(own_key, shape, width, limit, split=(), kind=jnp.bfloat16):
    loudness = levels(own_key, shape, split, -0.22, 0.18) if split else 1.0
    array = jax.random.normal(own_key, shape, jnp.float32) * width * loudness
    return jnp.minimum(jnp.maximum(array, -limit), limit).astype(kind)


def setup_inputs(seed: int = 0) -> dict:
    seeds = jax.random.split(jax.random.key(seed), 13)
    tokens = normal_values(seeds[0], (TOKENS, D), 1.0, 6.0, ((0, 32),))
    cotangent = normal_values(seeds[1], (TOKENS, D), 1.0, 6.0, ((0, 32),))
    segment_ids = jax.vmap(lambda own: jnp.searchsorted(jnp.cumsum(uneven(own, 4, SEQ_LEN, SEQ_LEN // 2, 1)), jnp.arange(SEQ_LEN), side="right"))(jax.random.split(seeds[2], SEQS)).reshape((SEQS, SEQ_LEN)).astype(jnp.int32)
    tract_order = jax.vmap(lambda own: jax.random.permutation(own, STRETCHES))(jax.random.split(seeds[3], SEQS)).reshape((SEQS, STRETCHES)).astype(jnp.int32)
    qkv_weight = normal_values(seeds[4], (D, 3 * D), D ** -0.5, 0.1875, ((0, 32),))
    out_weight = normal_values(seeds[5], (D, D), (D // 128) ** -0.5, 2.0, ((0, 32),))
    up_weight = normal_values(seeds[6], (D, FF), D ** -0.5, 0.1875, ((0, 32),))
    down_weight = normal_values(seeds[7], (FF, D), FF ** -0.5, 0.09375, ((0, 32),))
    norm_gain = jnp.clip(1.0 + 0.1 * jax.random.normal(seeds[8], (2, D), jnp.float32), 0.5, 1.5).astype(jnp.bfloat16)
    norm_shift = normal_values(seeds[9], (2, D), 0.3, 4.0, ((1, 32),))
    proj_bias = normal_values(seeds[10], (4, D), 0.5, 6.0, ((1, 32),))
    up_bias = normal_values(seeds[11], (FF,), 0.5, 6.0, ((0, 32),))
    return {"tokens": tokens, "cotangent": cotangent, "segment_ids": segment_ids, "tract_order": tract_order, "qkv_weight": qkv_weight, "out_weight": out_weight, "up_weight": up_weight, "down_weight": down_weight, "norm_gain": norm_gain, "norm_shift": norm_shift, "proj_bias": proj_bias, "up_bias": up_bias}


EPSILON = 1e-05
GELU_COEF = 0.7978845608028654

def rounded(values):
    return lax.optimization_barrier(values.astype(jnp.bfloat16)).astype(jnp.float32)

def gelu_parts(inputs):
    cubed_part = inputs * inputs * inputs
    tanh_part = jnp.tanh(GELU_COEF * (inputs + 0.044715 * cubed_part))
    values = 0.5 * inputs * (1.0 + tanh_part)
    slopes = 0.5 * (1.0 + tanh_part) + 0.5 * inputs * (1.0 - tanh_part * tanh_part) * GELU_COEF * (1.0 + 3.0 * 0.044715 * inputs * inputs)
    return (values, slopes)

def norm_parts(values):
    centred = values - lax.optimization_barrier(jnp.mean(values, axis=-1, keepdims=True))
    inverse = lax.rsqrt(lax.optimization_barrier(jnp.mean(centred * centred, axis=-1, keepdims=True)) + EPSILON)
    return (centred * inverse, inverse)

def norm_back(grads, normed, inverse, gain_row):
    scaled = grads * gain_row
    return inverse * (scaled - lax.optimization_barrier(jnp.mean(scaled, axis=-1, keepdims=True)) - normed * lax.optimization_barrier(jnp.mean(scaled * normed, axis=-1, keepdims=True)))

def reference(tokens, cotangent, segment_ids, tract_order, qkv_weight, out_weight, up_weight, down_weight, norm_gain, norm_shift, proj_bias, up_bias):
    gains = norm_gain.astype(jnp.float32)
    shifts = norm_shift.astype(jnp.float32)
    biases = proj_bias.astype(jnp.float32)
    up_shift = up_bias.astype(jnp.float32)
    attn_scale = HEAD_DIM ** (-0.5)

    def one_sequence(totals, inputs):
        hidden_in, grad_out, seg_row, block_ranks = inputs
        positions = (block_ranks[:, None] * STRETCH + jnp.arange(STRETCH, dtype=jnp.int32)[None, :]).reshape(-1)
        segments = jnp.take(seg_row.reshape(STRETCHES, STRETCH), block_ranks, axis=0).reshape(-1)
        allowed = (positions[None, :] <= positions[:, None]) & (segments[None, :] == segments[:, None])
        resid_in = hidden_in.astype(jnp.float32)
        normed_one, inverse_one = norm_parts(resid_in)
        normed_in = (normed_one * gains[0] + shifts[0]).astype(jnp.bfloat16)
        projected = jnp.dot(normed_in, qkv_weight, preferred_element_type=jnp.float32)
        query_rows = (projected[:, :D] + biases[0]).astype(jnp.bfloat16)
        key_rows = projected[:, D:2 * D].astype(jnp.bfloat16)
        value_rows = (projected[:, 2 * D:] + biases[1]).astype(jnp.bfloat16)
        query_heads = query_rows.astype(jnp.float32).reshape(SEQ_LEN, HEADS, HEAD_DIM)
        key_heads = key_rows.astype(jnp.float32).reshape(SEQ_LEN, HEADS, HEAD_DIM)
        value_heads = value_rows.astype(jnp.float32).reshape(SEQ_LEN, HEADS, HEAD_DIM)
        scores = jnp.einsum('qhd,khd->hqk', query_heads, key_heads) * attn_scale
        exp_weights = jnp.where(allowed[None], jnp.exp(scores), 0.0)
        denominator = lax.optimization_barrier(jnp.sum(exp_weights, axis=-1))
        numerator = jnp.einsum('hqk,khd->qhd', rounded(exp_weights), value_heads)
        attended = (numerator / denominator.T[:, :, None]).reshape(SEQ_LEN, D).astype(jnp.bfloat16)
        log_total = jnp.log(denominator)
        resid_mid = resid_in + jnp.dot(attended, out_weight, preferred_element_type=jnp.float32) + biases[2]
        normed_two, inverse_two = norm_parts(resid_mid)
        normed_mid = (normed_two * gains[1] + shifts[1]).astype(jnp.bfloat16)
        pre_act = jnp.dot(normed_mid, up_weight, preferred_element_type=jnp.float32) + up_shift
        activated, slopes = gelu_parts(pre_act)
        act_rows = activated.astype(jnp.bfloat16)
        resid_out = resid_mid + jnp.dot(act_rows, down_weight, preferred_element_type=jnp.float32) + biases[3]
        grad_top = grad_out.astype(jnp.float32)
        grad_down = jnp.dot(act_rows.T, grad_out, preferred_element_type=jnp.float32)
        grad_act = jnp.dot(grad_out, down_weight.T, preferred_element_type=jnp.float32)
        grad_pre = grad_act * slopes
        grad_pre_low = grad_pre.astype(jnp.bfloat16)
        grad_up = jnp.dot(normed_mid.T, grad_pre_low, preferred_element_type=jnp.float32)
        grad_norm_two = jnp.dot(grad_pre_low, up_weight.T, preferred_element_type=jnp.float32)
        grad_mid = grad_top + norm_back(grad_norm_two, normed_two, inverse_two, gains[1])
        grad_mid_low = grad_mid.astype(jnp.bfloat16)
        grad_outw = jnp.dot(attended.T, grad_mid_low, preferred_element_type=jnp.float32)
        grad_att = jnp.dot(grad_mid_low, out_weight.T, preferred_element_type=jnp.float32).astype(jnp.bfloat16)
        grad_att_heads = grad_att.astype(jnp.float32).reshape(SEQ_LEN, HEADS, HEAD_DIM)
        att_heads = attended.astype(jnp.float32).reshape(SEQ_LEN, HEADS, HEAD_DIM)
        delta_rows = lax.optimization_barrier(jnp.sum(grad_att_heads * att_heads, axis=-1)).T
        soft_weights = jnp.where(allowed[None], jnp.exp(scores - log_total[:, :, None]), 0.0)
        grad_value = jnp.einsum('hqk,qhd->khd', rounded(soft_weights), grad_att_heads).reshape(SEQ_LEN, D)
        grad_probs = jnp.einsum('qhd,khd->hqk', grad_att_heads, value_heads)
        grad_scores = rounded(soft_weights * (grad_probs - delta_rows[:, :, None]))
        grad_query = jnp.einsum('hqk,khd->qhd', grad_scores, key_heads).reshape(SEQ_LEN, D) * attn_scale
        grad_key = jnp.einsum('hqk,qhd->khd', grad_scores, query_heads).reshape(SEQ_LEN, D) * attn_scale
        grad_proj = jnp.concatenate([grad_query, grad_key, grad_value], axis=1).astype(jnp.bfloat16)
        grad_qkv = jnp.dot(normed_in.T, grad_proj, preferred_element_type=jnp.float32)
        grad_norm_one = jnp.dot(grad_proj, qkv_weight.T, preferred_element_type=jnp.float32)
        grad_in = grad_mid + norm_back(grad_norm_one, normed_one, inverse_one, gains[0])
        grad_gain = jnp.stack([lax.optimization_barrier(jnp.sum(grad_norm_one * normed_one, axis=0)), lax.optimization_barrier(jnp.sum(grad_norm_two * normed_two, axis=0))])
        grad_shift = jnp.stack([lax.optimization_barrier(jnp.sum(grad_norm_one, axis=0)), lax.optimization_barrier(jnp.sum(grad_norm_two, axis=0))])
        grad_bias = jnp.stack([lax.optimization_barrier(jnp.sum(grad_query, axis=0)), lax.optimization_barrier(jnp.sum(grad_value, axis=0)), lax.optimization_barrier(jnp.sum(grad_mid, axis=0)), lax.optimization_barrier(jnp.sum(grad_top, axis=0))])
        grad_upb = lax.optimization_barrier(jnp.sum(grad_pre, axis=0))
        fresh = (grad_qkv, grad_outw, grad_up, grad_down, grad_gain, grad_shift, grad_bias, grad_upb)
        summed = jax.tree.map(lambda former, latter: former + latter, totals, fresh)
        return (summed, (resid_out, grad_in))
    start_totals = (jnp.zeros((D, 3 * D), jnp.float32), jnp.zeros((D, D), jnp.float32), jnp.zeros((D, FF), jnp.float32), jnp.zeros((FF, D), jnp.float32), jnp.zeros((2, D), jnp.float32), jnp.zeros((2, D), jnp.float32), jnp.zeros((4, D), jnp.float32), jnp.zeros((FF,), jnp.float32))
    seq_tokens = tokens.reshape(SEQS, SEQ_LEN, D)
    seq_grads = cotangent.reshape(SEQS, SEQ_LEN, D)
    totals, outputs = lax.scan(one_sequence, start_totals, (seq_tokens, seq_grads, segment_ids, tract_order))
    block_out = outputs[0].reshape(TOKENS, D)
    input_grad = outputs[1].reshape(TOKENS, D)
    return (block_out, input_grad, totals[0], totals[1], totals[2], totals[3], totals[4], totals[5], totals[6], totals[7])
```

```python
import jax
import jax.numpy as jnp
from jax import lax
from jax.sharding import PartitionSpec as P

HEAD_DIM = 64


EPSILON = 1e-05
GELU_COEF = 0.7978845608028654


def gelu_parts(inputs):
    cubed_part = inputs * inputs * inputs
    tanh_part = jnp.tanh(GELU_COEF * (inputs + 0.044715 * cubed_part))
    values = 0.5 * inputs * (1.0 + tanh_part)
    slopes = 0.5 * (1.0 + tanh_part) + 0.5 * inputs * (1.0 - tanh_part * tanh_part) * GELU_COEF * (
        1.0 + 3.0 * 0.044715 * inputs * inputs
    )
    return (values, slopes)


def norm_parts(values):
    centred = values - jnp.mean(values, axis=-1, keepdims=True)
    inverse = lax.rsqrt(jnp.mean(centred * centred, axis=-1, keepdims=True) + EPSILON)
    return (centred * inverse, inverse)


def norm_back(grads, normed, inverse, gain_row):
    scaled = grads * gain_row
    return inverse * (
        scaled
        - jnp.mean(scaled, axis=-1, keepdims=True)
        - normed * jnp.mean(scaled * normed, axis=-1, keepdims=True)
    )


def outer_sum(former, latter):
    return lax.dot_general(
        former, latter, (((0,), (0,)), ((), ())), preferred_element_type=jnp.float32
    )


def back_product(former, latter):
    return lax.dot_general(
        former, latter, (((1,), (1,)), ((), ())), preferred_element_type=jnp.float32
    )


def shards(
    tokens,
    cotangent,
    segment_ids,
    tract_order,
    qkv_weight,
    out_weight,
    up_weight,
    down_weight,
    norm_gain,
    norm_shift,
    proj_bias,
    up_bias,
):
    both = ("dp", "ctx")
    dp_count = lax.axis_size("dp")
    ctx_count = lax.axis_size("ctx")
    here = lax.axis_index("ctx")
    row_count, width = tokens.shape
    span = row_count * ctx_count
    block_rows = segment_ids.shape[1] // tract_order.shape[1]
    own_rows = qkv_weight.shape[0]
    own_hidden = up_bias.shape[0]
    own_feats = norm_gain.shape[1]
    hidden = dp_count * own_hidden
    part = width // ctx_count
    heads = part // HEAD_DIM
    attn_scale = HEAD_DIM ** (-0.5)

    smalls = jnp.concatenate(
        [norm_gain.reshape(-1), norm_shift.reshape(-1), proj_bias.reshape(-1), up_bias]
    )[None]
    smalls = lax.all_gather(smalls, both, axis=0, tiled=True).astype(jnp.float32)

    def spread(first, count):
        piece = smalls[:, first * own_feats : (first + count) * own_feats]
        return piece.reshape(-1, count, own_feats).transpose(1, 0, 2).reshape(count, width)

    gains = spread(0, 2)
    shifts = spread(2, 2)
    biases = spread(4, 4)
    up_shift = lax.dynamic_index_in_dim(
        smalls[:, 8 * own_feats :].reshape(dp_count, ctx_count, own_hidden), here, 1, False
    ).reshape(hidden)

    qkv_cols = (
        qkv_weight.reshape(own_rows, 3, ctx_count, part)
        .transpose(2, 0, 1, 3)
        .reshape(ctx_count, own_rows, 3 * part)
    )
    up_cols = (
        up_weight.reshape(own_rows, dp_count, ctx_count, own_hidden)
        .transpose(2, 0, 1, 3)
        .reshape(ctx_count, own_rows, hidden)
    )
    swapped = lax.all_to_all(
        jnp.concatenate([qkv_cols, up_cols], axis=2), "ctx", 0, 0, tiled=True
    ).reshape(ctx_count * own_rows, 3 * part + hidden)
    streams = lax.all_gather(jnp.stack([tokens, cotangent]), "ctx", axis=1, tiled=True)
    qkv_part = lax.all_gather(swapped[:, : 3 * part], "dp", axis=0, tiled=True)
    out_full = lax.all_gather(out_weight, both, axis=0, tiled=True)
    up_part = lax.all_gather(swapped[:, 3 * part :], "dp", axis=0, tiled=True)
    down_part = lax.all_gather(down_weight, "dp", axis=0, tiled=True)
    tokens_span, cot_span = streams[0], streams[1]

    block_ranks = tract_order[0]
    positions = (
        block_ranks[:, None] * block_rows + jnp.arange(block_rows, dtype=jnp.int32)[None, :]
    ).reshape(-1)
    segments = jnp.take(segment_ids[0].reshape(-1, block_rows), block_ranks, axis=0).reshape(-1)
    allowed = (positions[None, :] <= positions[:, None]) & (
        segments[None, :] == segments[:, None]
    )

    normed_span, _ = norm_parts(tokens_span.astype(jnp.float32))
    normed_in = (normed_span * gains[0] + shifts[0]).astype(jnp.bfloat16)
    projected = jnp.dot(normed_in, qkv_part, preferred_element_type=jnp.float32)
    query_shift = lax.dynamic_slice_in_dim(biases[0], here * part, part)
    value_shift = lax.dynamic_slice_in_dim(biases[1], here * part, part)
    query_heads = (
        (projected[:, :part] + query_shift).astype(jnp.bfloat16).reshape(span, heads, HEAD_DIM)
    )
    key_heads = projected[:, part : 2 * part].astype(jnp.bfloat16).reshape(span, heads, HEAD_DIM)
    value_heads = (
        (projected[:, 2 * part :] + value_shift).astype(jnp.bfloat16).reshape(span, heads, HEAD_DIM)
    )
    scores = (
        jnp.einsum("qhd,khd->hqk", query_heads, key_heads, preferred_element_type=jnp.float32)
        * attn_scale
    )
    exp_weights = jnp.where(allowed[None], jnp.exp(scores), 0.0)
    denominator = jnp.sum(exp_weights, axis=-1)
    numerator = jnp.einsum(
        "hqk,khd->qhd",
        exp_weights.astype(jnp.bfloat16),
        value_heads,
        preferred_element_type=jnp.float32,
    )
    att_heads = (numerator / denominator.T[:, :, None]).astype(jnp.bfloat16)
    log_total = jnp.log(denominator)
    att_part = att_heads.reshape(span, part)
    attended = lax.all_to_all(att_part, "ctx", 0, 1, tiled=True)

    resid_in = tokens.astype(jnp.float32)
    resid_mid = (
        resid_in + jnp.dot(attended, out_full, preferred_element_type=jnp.float32) + biases[2]
    )
    normed_two, inverse_two = norm_parts(resid_mid)
    normed_mid = lax.all_gather(
        (normed_two * gains[1] + shifts[1]).astype(jnp.bfloat16), "ctx", axis=0, tiled=True
    )
    pre_act = jnp.dot(normed_mid, up_part, preferred_element_type=jnp.float32) + up_shift
    activated, slopes = gelu_parts(pre_act)
    act_rows = activated.astype(jnp.bfloat16)

    grad_top = cotangent.astype(jnp.float32)
    grad_act = back_product(cot_span, down_part)
    grad_pre = grad_act * slopes
    grad_pre_low = grad_pre.astype(jnp.bfloat16)
    grad_norm_two = lax.psum_scatter(
        back_product(grad_pre_low, up_part).astype(jnp.bfloat16),
        "ctx",
        scatter_dimension=0,
        tiled=True,
    ).astype(jnp.float32)
    block_out = (
        resid_mid
        + lax.psum_scatter(
            jnp.dot(act_rows, down_part, preferred_element_type=jnp.float32).astype(jnp.bfloat16),
            "ctx",
            scatter_dimension=0,
            tiled=True,
        ).astype(jnp.float32)
        + biases[3]
    )
    grad_mid = grad_top + norm_back(grad_norm_two, normed_two, inverse_two, gains[1])
    mid_span = lax.all_gather(grad_mid.astype(jnp.bfloat16), "ctx", axis=0, tiled=True)
    out_rows = lax.dynamic_slice_in_dim(out_full, here * part, part)
    grad_att = back_product(mid_span, out_rows).astype(jnp.bfloat16).reshape(span, heads, HEAD_DIM)
    delta_rows = jnp.sum(
        grad_att.astype(jnp.float32) * att_heads.astype(jnp.float32), axis=-1
    ).T
    soft_weights = jnp.where(allowed[None], jnp.exp(scores - log_total[:, :, None]), 0.0)
    grad_value = jnp.einsum(
        "hqk,qhd->khd",
        soft_weights.astype(jnp.bfloat16),
        grad_att,
        preferred_element_type=jnp.float32,
    ).reshape(span, part)
    grad_probs = jnp.einsum(
        "qhd,khd->hqk", grad_att, value_heads, preferred_element_type=jnp.float32
    )
    grad_scores = (soft_weights * (grad_probs - delta_rows[:, :, None])).astype(jnp.bfloat16)
    grad_query = (
        jnp.einsum(
            "hqk,khd->qhd", grad_scores, key_heads, preferred_element_type=jnp.float32
        ).reshape(span, part)
        * attn_scale
    )
    grad_key = (
        jnp.einsum(
            "hqk,qhd->khd", grad_scores, query_heads, preferred_element_type=jnp.float32
        ).reshape(span, part)
        * attn_scale
    )
    grad_proj = jnp.concatenate([grad_query, grad_key, grad_value], axis=1).astype(jnp.bfloat16)
    grad_norm_one = lax.psum_scatter(
        back_product(grad_proj, qkv_part).astype(jnp.bfloat16),
        "ctx",
        scatter_dimension=0,
        tiled=True,
    ).astype(jnp.float32)
    normed_one, inverse_one = norm_parts(resid_in)
    input_grad = grad_mid + norm_back(grad_norm_one, normed_one, inverse_one, gains[0])

    def over_dp(former, latter):
        return lax.psum_scatter(
            outer_sum(former, latter).astype(jnp.bfloat16), "dp", scatter_dimension=0, tiled=True
        )

    down_grad = over_dp(act_rows, cot_span).astype(jnp.float32)
    up_rows = over_dp(normed_mid, grad_pre_low)
    outw_rows = over_dp(att_part, mid_span)
    qkv_rows = over_dp(normed_in, grad_proj)
    outw_grad = lax.ppermute(
        outw_rows,
        both,
        [
            (d * ctx_count + c, c * dp_count + d)
            for d in range(dp_count)
            for c in range(ctx_count)
        ],
    ).astype(jnp.float32)
    returned = lax.all_to_all(
        jnp.concatenate([qkv_rows, up_rows], axis=1).reshape(ctx_count, own_rows, -1),
        "ctx",
        0,
        0,
        tiled=True,
    ).astype(jnp.float32)
    qkv_grad = (
        returned[:, :, : 3 * part]
        .reshape(ctx_count, own_rows, 3, part)
        .transpose(1, 2, 0, 3)
        .reshape(own_rows, 3 * width)
    )
    up_grad = (
        returned[:, :, 3 * part :]
        .reshape(ctx_count, own_rows, dp_count, own_hidden)
        .transpose(1, 2, 0, 3)
        .reshape(own_rows, hidden * ctx_count)
    )

    def placed(sums):
        return lax.dynamic_update_slice_in_dim(
            jnp.zeros((width,), jnp.float32), sums, here * part, 0
        )

    feature_sums = jnp.stack(
        [
            jnp.sum(grad_norm_one * normed_one, axis=0),
            jnp.sum(grad_norm_two * normed_two, axis=0),
            jnp.sum(grad_norm_one, axis=0),
            jnp.sum(grad_norm_two, axis=0),
            placed(jnp.sum(grad_query, axis=0)),
            placed(jnp.sum(grad_value, axis=0)),
            jnp.sum(grad_mid, axis=0),
            jnp.sum(grad_top, axis=0),
        ]
    )
    hidden_sums = lax.dynamic_update_slice_in_dim(
        jnp.zeros((dp_count, ctx_count, own_hidden), jnp.float32),
        jnp.sum(grad_pre, axis=0).reshape(dp_count, 1, own_hidden),
        here,
        1,
    ).reshape(dp_count * ctx_count, own_hidden)
    packed = jnp.concatenate(
        [
            feature_sums.reshape(8, -1, own_feats).transpose(1, 0, 2).reshape(-1, 8 * own_feats),
            hidden_sums,
        ],
        axis=1,
    )
    owned = lax.psum_scatter(packed, both, scatter_dimension=0, tiled=True)[0]
    rows = owned[: 8 * own_feats].reshape(8, own_feats)
    return (
        block_out,
        input_grad,
        qkv_grad,
        outw_grad,
        up_grad,
        down_grad,
        rows[0:2],
        rows[2:4],
        rows[4:8],
        owned[8 * own_feats :],
    )


def solution(mesh):
    return jax.shard_map(
        shards,
        mesh=mesh,
        in_specs=(
            P(("dp", "ctx"), None),
            P(("dp", "ctx"), None),
            P("dp", None),
            P("dp", None),
            P(("dp", "ctx"), None),
            P(("dp", "ctx"), None),
            P(("dp", "ctx"), None),
            P(("dp", "ctx"), None),
            P(None, ("dp", "ctx")),
            P(None, ("dp", "ctx")),
            P(None, ("dp", "ctx")),
            P(("dp", "ctx")),
        ),
        out_specs=(
            P(("dp", "ctx"), None),
            P(("dp", "ctx"), None),
            P(("dp", "ctx"), None),
            P(("dp", "ctx"), None),
            P(("dp", "ctx"), None),
            P(("dp", "ctx"), None),
            P(None, ("dp", "ctx")),
            P(None, ("dp", "ctx")),
            P(None, ("dp", "ctx")),
            P(("dp", "ctx")),
        ),
        check_vma=False,
    )
```

```python
import jax
import jax.numpy as jnp
from jax import lax
from jax.sharding import PartitionSpec as P

HEAD_DIM = 64


EPSILON = 1e-05
GELU_COEF = 0.7978845608028654


def gelu_parts(inputs):
    cubed_part = inputs * inputs * inputs
    tanh_part = jnp.tanh(GELU_COEF * (inputs + 0.044715 * cubed_part))
    values = 0.5 * inputs * (1.0 + tanh_part)
    slopes = 0.5 * (1.0 + tanh_part) + 0.5 * inputs * (1.0 - tanh_part * tanh_part) * GELU_COEF * (
        1.0 + 3.0 * 0.044715 * inputs * inputs
    )
    return (values, slopes)


def norm_parts(values):
    centred = values - jnp.mean(values, axis=-1, keepdims=True)
    inverse = lax.rsqrt(jnp.mean(centred * centred, axis=-1, keepdims=True) + EPSILON)
    return (centred * inverse, inverse)


def norm_back(grads, normed, inverse, gain_row):
    scaled = grads * gain_row
    return inverse * (
        scaled
        - jnp.mean(scaled, axis=-1, keepdims=True)
        - normed * jnp.mean(scaled * normed, axis=-1, keepdims=True)
    )


def outer_sum(former, latter):
    return lax.dot_general(
        former, latter, (((0,), (0,)), ((), ())), preferred_element_type=jnp.float32
    )


def back_product(former, latter):
    return lax.dot_general(
        former, latter, (((1,), (1,)), ((), ())), preferred_element_type=jnp.float32
    )


def shared(rows, axis, count):
    spread_rows = jnp.broadcast_to(rows[None], (count,) + rows.shape)
    return lax.all_to_all(spread_rows, axis, 0, 0, tiled=True).reshape((-1,) + rows.shape[1:])


def summed(partial, axis, count):
    parts = lax.all_to_all(partial, axis, 0, 0, tiled=True)
    return jnp.sum(parts.reshape((count, -1) + partial.shape[1:]).astype(jnp.float32), axis=0)


def shards(
    tokens,
    cotangent,
    segment_ids,
    tract_order,
    qkv_weight,
    out_weight,
    up_weight,
    down_weight,
    norm_gain,
    norm_shift,
    proj_bias,
    up_bias,
):
    both = ("dp", "ctx")
    dp_count = lax.axis_size("dp")
    ctx_count = lax.axis_size("ctx")
    here = lax.axis_index("ctx")
    row_count, width = tokens.shape
    span = row_count * ctx_count
    block_rows = segment_ids.shape[1] // tract_order.shape[1]
    own_rows = qkv_weight.shape[0]
    own_hidden = up_bias.shape[0]
    own_feats = norm_gain.shape[1]
    hidden = dp_count * own_hidden
    part = width // ctx_count
    heads = part // HEAD_DIM
    attn_scale = HEAD_DIM ** (-0.5)

    smalls = jnp.concatenate(
        [norm_gain.reshape(-1), norm_shift.reshape(-1), proj_bias.reshape(-1), up_bias]
    )[None]
    smalls = shared(smalls, both, dp_count * ctx_count).astype(jnp.float32)

    def spread(first, count):
        piece = smalls[:, first * own_feats : (first + count) * own_feats]
        return piece.reshape(-1, count, own_feats).transpose(1, 0, 2).reshape(count, width)

    gains = spread(0, 2)
    shifts = spread(2, 2)
    biases = spread(4, 4)
    up_shift = lax.dynamic_index_in_dim(
        smalls[:, 8 * own_feats :].reshape(dp_count, ctx_count, own_hidden), here, 1, False
    ).reshape(hidden)

    qkv_cols = (
        qkv_weight.reshape(own_rows, 3, ctx_count, part)
        .transpose(2, 0, 1, 3)
        .reshape(ctx_count, own_rows, 3 * part)
    )
    up_cols = (
        up_weight.reshape(own_rows, dp_count, ctx_count, own_hidden)
        .transpose(2, 0, 1, 3)
        .reshape(ctx_count, own_rows, hidden)
    )
    swapped = lax.all_to_all(
        jnp.concatenate([qkv_cols, up_cols], axis=2), "ctx", 0, 0, tiled=True
    ).reshape(ctx_count * own_rows, 3 * part + hidden)
    tokens_span = shared(tokens, "ctx", ctx_count)
    cot_span = shared(cotangent, "ctx", ctx_count)
    qkv_part = shared(swapped[:, : 3 * part], "dp", dp_count)
    out_part = lax.all_gather(out_weight, "dp", axis=0, tiled=True)
    out_full = (
        shared(out_part, "ctx", ctx_count)
        .reshape(ctx_count, dp_count, own_rows, width)
        .transpose(1, 0, 2, 3)
        .reshape(width, width)
    )
    up_part = lax.all_gather(swapped[:, 3 * part :], "dp", axis=0, tiled=True)
    down_part = lax.all_gather(down_weight, "dp", axis=0, tiled=True)

    block_ranks = tract_order[0]
    positions = (
        block_ranks[:, None] * block_rows + jnp.arange(block_rows, dtype=jnp.int32)[None, :]
    ).reshape(-1)
    segments = jnp.take(segment_ids[0].reshape(-1, block_rows), block_ranks, axis=0).reshape(-1)
    allowed = (positions[None, :] <= positions[:, None]) & (
        segments[None, :] == segments[:, None]
    )

    normed_span, _ = norm_parts(tokens_span.astype(jnp.float32))
    normed_in = (normed_span * gains[0] + shifts[0]).astype(jnp.bfloat16)
    projected = jnp.dot(normed_in, qkv_part, preferred_element_type=jnp.float32)
    query_shift = lax.dynamic_slice_in_dim(biases[0], here * part, part)
    value_shift = lax.dynamic_slice_in_dim(biases[1], here * part, part)
    query_heads = (
        (projected[:, :part] + query_shift).astype(jnp.bfloat16).reshape(span, heads, HEAD_DIM)
    )
    key_heads = projected[:, part : 2 * part].astype(jnp.bfloat16).reshape(span, heads, HEAD_DIM)
    value_heads = (
        (projected[:, 2 * part :] + value_shift).astype(jnp.bfloat16).reshape(span, heads, HEAD_DIM)
    )
    scores = (
        jnp.einsum("qhd,khd->hqk", query_heads, key_heads, preferred_element_type=jnp.float32)
        * attn_scale
    )
    exp_weights = jnp.where(allowed[None], jnp.exp(scores), 0.0)
    denominator = jnp.sum(exp_weights, axis=-1)
    numerator = jnp.einsum(
        "hqk,khd->qhd",
        exp_weights.astype(jnp.bfloat16),
        value_heads,
        preferred_element_type=jnp.float32,
    )
    att_heads = (numerator / denominator.T[:, :, None]).astype(jnp.bfloat16)
    log_total = jnp.log(denominator)
    att_part = att_heads.reshape(span, part)
    attended = lax.all_to_all(att_part, "ctx", 0, 1, tiled=True)

    resid_in = tokens.astype(jnp.float32)
    resid_mid = (
        resid_in + jnp.dot(attended, out_full, preferred_element_type=jnp.float32) + biases[2]
    )
    normed_two, inverse_two = norm_parts(resid_mid)
    normed_mid = shared(
        (normed_two * gains[1] + shifts[1]).astype(jnp.bfloat16), "ctx", ctx_count
    )
    pre_act = jnp.dot(normed_mid, up_part, preferred_element_type=jnp.float32) + up_shift
    activated, slopes = gelu_parts(pre_act)
    act_rows = activated.astype(jnp.bfloat16)

    grad_top = cotangent.astype(jnp.float32)
    grad_act = back_product(cot_span, down_part)
    grad_pre = grad_act * slopes
    grad_pre_low = grad_pre.astype(jnp.bfloat16)
    grad_norm_two = summed(
        back_product(grad_pre_low, up_part).astype(jnp.bfloat16), "ctx", ctx_count
    )
    block_out = (
        resid_mid
        + summed(
            jnp.dot(act_rows, down_part, preferred_element_type=jnp.float32).astype(jnp.bfloat16),
            "ctx",
            ctx_count,
        )
        + biases[3]
    )
    grad_mid = grad_top + norm_back(grad_norm_two, normed_two, inverse_two, gains[1])
    mid_span = shared(grad_mid.astype(jnp.bfloat16), "ctx", ctx_count)
    out_rows = lax.dynamic_slice_in_dim(out_full, here * part, part)
    grad_att = back_product(mid_span, out_rows).astype(jnp.bfloat16).reshape(span, heads, HEAD_DIM)
    delta_rows = jnp.sum(
        grad_att.astype(jnp.float32) * att_heads.astype(jnp.float32), axis=-1
    ).T
    soft_weights = jnp.where(allowed[None], jnp.exp(scores - log_total[:, :, None]), 0.0)
    grad_value = jnp.einsum(
        "hqk,qhd->khd",
        soft_weights.astype(jnp.bfloat16),
        grad_att,
        preferred_element_type=jnp.float32,
    ).reshape(span, part)
    grad_probs = jnp.einsum(
        "qhd,khd->hqk", grad_att, value_heads, preferred_element_type=jnp.float32
    )
    grad_scores = (soft_weights * (grad_probs - delta_rows[:, :, None])).astype(jnp.bfloat16)
    grad_query = (
        jnp.einsum(
            "hqk,khd->qhd", grad_scores, key_heads, preferred_element_type=jnp.float32
        ).reshape(span, part)
        * attn_scale
    )
    grad_key = (
        jnp.einsum(
            "hqk,qhd->khd", grad_scores, query_heads, preferred_element_type=jnp.float32
        ).reshape(span, part)
        * attn_scale
    )
    grad_proj = jnp.concatenate([grad_query, grad_key, grad_value], axis=1).astype(jnp.bfloat16)
    grad_norm_one = summed(
        back_product(grad_proj, qkv_part).astype(jnp.bfloat16), "ctx", ctx_count
    )
    normed_one, inverse_one = norm_parts(resid_in)
    input_grad = grad_mid + norm_back(grad_norm_one, normed_one, inverse_one, gains[0])

    def over_dp(former, latter):
        return lax.psum_scatter(
            outer_sum(former, latter).astype(jnp.bfloat16), "dp", scatter_dimension=0, tiled=True
        )

    down_grad = over_dp(act_rows, cot_span).astype(jnp.float32)
    up_rows = summed(
        outer_sum(normed_mid, grad_pre_low).astype(jnp.bfloat16), "dp", dp_count
    ).astype(jnp.bfloat16)
    outw_rows = over_dp(att_part, mid_span)
    qkv_rows = summed(
        outer_sum(normed_in, grad_proj).astype(jnp.bfloat16), "dp", dp_count
    ).astype(jnp.bfloat16)
    outw_grad = lax.ppermute(
        outw_rows,
        both,
        [
            (d * ctx_count + c, c * dp_count + d)
            for d in range(dp_count)
            for c in range(ctx_count)
        ],
    ).astype(jnp.float32)
    returned = lax.all_to_all(
        jnp.concatenate([qkv_rows, up_rows], axis=1).reshape(ctx_count, own_rows, -1),
        "ctx",
        0,
        0,
        tiled=True,
    ).astype(jnp.float32)
    qkv_grad = (
        returned[:, :, : 3 * part]
        .reshape(ctx_count, own_rows, 3, part)
        .transpose(1, 2, 0, 3)
        .reshape(own_rows, 3 * width)
    )
    up_grad = (
        returned[:, :, 3 * part :]
        .reshape(ctx_count, own_rows, dp_count, own_hidden)
        .transpose(1, 2, 0, 3)
        .reshape(own_rows, hidden * ctx_count)
    )

    def placed(sums):
        return lax.dynamic_update_slice_in_dim(
            jnp.zeros((width,), jnp.float32), sums, here * part, 0
        )

    feature_sums = jnp.stack(
        [
            jnp.sum(grad_norm_one * normed_one, axis=0),
            jnp.sum(grad_norm_two * normed_two, axis=0),
            jnp.sum(grad_norm_one, axis=0),
            jnp.sum(grad_norm_two, axis=0),
            placed(jnp.sum(grad_query, axis=0)),
            placed(jnp.sum(grad_value, axis=0)),
            jnp.sum(grad_mid, axis=0),
            jnp.sum(grad_top, axis=0),
        ]
    )
    hidden_sums = lax.dynamic_update_slice_in_dim(
        jnp.zeros((dp_count, ctx_count, own_hidden), jnp.float32),
        jnp.sum(grad_pre, axis=0).reshape(dp_count, 1, own_hidden),
        here,
        1,
    ).reshape(dp_count * ctx_count, own_hidden)
    packed = jnp.concatenate(
        [
            feature_sums.reshape(8, -1, own_feats).transpose(1, 0, 2).reshape(-1, 8 * own_feats),
            hidden_sums,
        ],
        axis=1,
    )
    owned = summed(packed, both, dp_count * ctx_count)[0]
    rows = owned[: 8 * own_feats].reshape(8, own_feats)
    return (
        block_out,
        input_grad,
        qkv_grad,
        outw_grad,
        up_grad,
        down_grad,
        rows[0:2],
        rows[2:4],
        rows[4:8],
        owned[8 * own_feats :],
    )


def solution(mesh):
    return jax.shard_map(
        shards,
        mesh=mesh,
        in_specs=(
            P(("dp", "ctx"), None),
            P(("dp", "ctx"), None),
            P("dp", None),
            P("dp", None),
            P(("dp", "ctx"), None),
            P(("dp", "ctx"), None),
            P(("dp", "ctx"), None),
            P(("dp", "ctx"), None),
            P(None, ("dp", "ctx")),
            P(None, ("dp", "ctx")),
            P(None, ("dp", "ctx")),
            P(("dp", "ctx")),
        ),
        out_specs=(
            P(("dp", "ctx"), None),
            P(("dp", "ctx"), None),
            P(("dp", "ctx"), None),
            P(("dp", "ctx"), None),
            P(("dp", "ctx"), None),
            P(("dp", "ctx"), None),
            P(None, ("dp", "ctx")),
            P(None, ("dp", "ctx")),
            P(None, ("dp", "ctx")),
            P(("dp", "ctx")),
        ),
        check_vma=False,
    )
```

```python
import jax
import jax.numpy as jnp
from jax import lax
from jax.sharding import PartitionSpec as P

HEAD_DIM = 64


EPSILON = 1e-05
GELU_COEF = 0.7978845608028654


def gelu_parts(inputs):
    cubed_part = inputs * inputs * inputs
    tanh_part = jnp.tanh(GELU_COEF * (inputs + 0.044715 * cubed_part))
    values = 0.5 * inputs * (1.0 + tanh_part)
    slopes = 0.5 * (1.0 + tanh_part) + 0.5 * inputs * (1.0 - tanh_part * tanh_part) * GELU_COEF * (
        1.0 + 3.0 * 0.044715 * inputs * inputs
    )
    return (values, slopes)


def norm_parts(values):
    centred = values - jnp.mean(values, axis=-1, keepdims=True)
    inverse = lax.rsqrt(jnp.mean(centred * centred, axis=-1, keepdims=True) + EPSILON)
    return (centred * inverse, inverse)


def norm_back(grads, normed, inverse, gain_row):
    scaled = grads * gain_row
    return inverse * (
        scaled
        - jnp.mean(scaled, axis=-1, keepdims=True)
        - normed * jnp.mean(scaled * normed, axis=-1, keepdims=True)
    )


def outer_sum(former, latter):
    return lax.dot_general(
        former, latter, (((0,), (0,)), ((), ())), preferred_element_type=jnp.float32
    )


def back_product(former, latter):
    return lax.dot_general(
        former, latter, (((1,), (1,)), ((), ())), preferred_element_type=jnp.float32
    )


def shared(rows, axis, count):
    spread_rows = jnp.broadcast_to(rows[None], (count,) + rows.shape)
    return lax.all_to_all(spread_rows, axis, 0, 0, tiled=True).reshape((-1,) + rows.shape[1:])


def summed(partial, axis, count):
    parts = lax.all_to_all(partial, axis, 0, 0, tiled=True)
    return jnp.sum(parts.reshape((count, -1) + partial.shape[1:]).astype(jnp.float32), axis=0)


def shards(
    tokens,
    cotangent,
    segment_ids,
    tract_order,
    qkv_weight,
    out_weight,
    up_weight,
    down_weight,
    norm_gain,
    norm_shift,
    proj_bias,
    up_bias,
):
    both = ("dp", "ctx")
    dp_count = lax.axis_size("dp")
    ctx_count = lax.axis_size("ctx")
    here = lax.axis_index("ctx")
    row_count, width = tokens.shape
    span = row_count * ctx_count
    block_rows = segment_ids.shape[1] // tract_order.shape[1]
    own_rows = qkv_weight.shape[0]
    own_hidden = up_bias.shape[0]
    own_feats = norm_gain.shape[1]
    hidden = dp_count * own_hidden
    part = width // ctx_count
    heads = part // HEAD_DIM
    attn_scale = HEAD_DIM ** (-0.5)

    smalls = jnp.concatenate(
        [norm_gain.reshape(-1), norm_shift.reshape(-1), proj_bias.reshape(-1), up_bias]
    )[None]
    smalls = shared(smalls, both, dp_count * ctx_count).astype(jnp.float32)

    def spread(first, count):
        piece = smalls[:, first * own_feats : (first + count) * own_feats]
        return piece.reshape(-1, count, own_feats).transpose(1, 0, 2).reshape(count, width)

    gains = spread(0, 2)
    shifts = spread(2, 2)
    biases = spread(4, 4)
    up_shift = lax.dynamic_index_in_dim(
        smalls[:, 8 * own_feats :].reshape(dp_count, ctx_count, own_hidden), here, 1, False
    ).reshape(hidden)

    qkv_cols = (
        qkv_weight.reshape(own_rows, 3, ctx_count, part)
        .transpose(2, 0, 1, 3)
        .reshape(ctx_count, own_rows, 3 * part)
    )
    up_cols = (
        up_weight.reshape(own_rows, dp_count, ctx_count, own_hidden)
        .transpose(2, 0, 1, 3)
        .reshape(ctx_count, own_rows, hidden)
    )
    swapped = lax.all_to_all(
        jnp.concatenate([qkv_cols, up_cols], axis=2), "ctx", 0, 0, tiled=True
    ).reshape(ctx_count * own_rows, 3 * part + hidden)
    tokens_span = shared(tokens, "ctx", ctx_count)
    cot_span = shared(cotangent, "ctx", ctx_count)
    qkv_part = shared(swapped[:, : 3 * part], "dp", dp_count)
    out_part = lax.all_gather(out_weight, "dp", axis=0, tiled=True)
    out_full = (
        shared(out_part, "ctx", ctx_count)
        .reshape(ctx_count, dp_count, own_rows, width)
        .transpose(1, 0, 2, 3)
        .reshape(width, width)
    )
    up_part = lax.all_gather(swapped[:, 3 * part :], "dp", axis=0, tiled=True)
    down_part = lax.all_gather(down_weight, "dp", axis=0, tiled=True)

    block_ranks = tract_order[0]
    positions = (
        block_ranks[:, None] * block_rows + jnp.arange(block_rows, dtype=jnp.int32)[None, :]
    ).reshape(-1)
    segments = jnp.take(segment_ids[0].reshape(-1, block_rows), block_ranks, axis=0).reshape(-1)
    allowed = (positions[None, :] <= positions[:, None]) & (
        segments[None, :] == segments[:, None]
    )

    normed_span, _ = norm_parts(tokens_span.astype(jnp.float32))
    normed_in = (normed_span * gains[0] + shifts[0]).astype(jnp.bfloat16)
    projected = jnp.dot(normed_in, qkv_part, preferred_element_type=jnp.float32)
    query_shift = lax.dynamic_slice_in_dim(biases[0], here * part, part)
    value_shift = lax.dynamic_slice_in_dim(biases[1], here * part, part)
    query_heads = (
        (projected[:, :part] + query_shift).astype(jnp.bfloat16).reshape(span, heads, HEAD_DIM)
    )
    key_heads = projected[:, part : 2 * part].astype(jnp.bfloat16).reshape(span, heads, HEAD_DIM)
    value_heads = (
        (projected[:, 2 * part :] + value_shift).astype(jnp.bfloat16).reshape(span, heads, HEAD_DIM)
    )
    scores = (
        jnp.einsum("qhd,khd->hqk", query_heads, key_heads, preferred_element_type=jnp.float32)
        * attn_scale
    )
    exp_weights = jnp.where(allowed[None], jnp.exp(scores), 0.0)
    denominator = jnp.sum(exp_weights, axis=-1)
    numerator = jnp.einsum(
        "hqk,khd->qhd",
        exp_weights.astype(jnp.bfloat16),
        value_heads,
        preferred_element_type=jnp.float32,
    )
    att_heads = (numerator / denominator.T[:, :, None]).astype(jnp.bfloat16)
    log_total = jnp.log(denominator)
    att_part = att_heads.reshape(span, part)
    attended = lax.all_to_all(att_part, "ctx", 0, 1, tiled=True)

    resid_in = tokens.astype(jnp.float32)
    resid_mid = (
        resid_in + jnp.dot(attended, out_full, preferred_element_type=jnp.float32) + biases[2]
    )
    normed_two, inverse_two = norm_parts(resid_mid)
    normed_mid = shared(
        (normed_two * gains[1] + shifts[1]).astype(jnp.bfloat16), "ctx", ctx_count
    )
    pre_act = jnp.dot(normed_mid, up_part, preferred_element_type=jnp.float32) + up_shift
    activated, slopes = gelu_parts(pre_act)
    act_rows = activated.astype(jnp.bfloat16)

    grad_top = cotangent.astype(jnp.float32)
    grad_act = back_product(cot_span, down_part)
    grad_pre = grad_act * slopes
    grad_pre_low = grad_pre.astype(jnp.bfloat16)
    down_product = outer_sum(act_rows, cot_span).astype(jnp.bfloat16)
    down_product, grad_pre_low = lax.optimization_barrier((down_product, grad_pre_low))
    down_grad = lax.psum_scatter(down_product, "dp", scatter_dimension=0, tiled=True)
    up_product = outer_sum(normed_mid, grad_pre_low).astype(jnp.bfloat16)
    grad_norm_two = summed(
        back_product(grad_pre_low, up_part).astype(jnp.bfloat16), "ctx", ctx_count
    )
    block_out = (
        resid_mid
        + summed(
            jnp.dot(act_rows, down_part, preferred_element_type=jnp.float32).astype(jnp.bfloat16),
            "ctx",
            ctx_count,
        )
        + biases[3]
    )
    up_product, grad_norm_two = lax.optimization_barrier((up_product, grad_norm_two))
    up_rows = lax.psum_scatter(up_product, "dp", scatter_dimension=0, tiled=True)
    grad_mid = grad_top + norm_back(grad_norm_two, normed_two, inverse_two, gains[1])
    mid_span = shared(grad_mid.astype(jnp.bfloat16), "ctx", ctx_count)
    out_rows = lax.dynamic_slice_in_dim(out_full, here * part, part)
    grad_att = back_product(mid_span, out_rows).astype(jnp.bfloat16).reshape(span, heads, HEAD_DIM)
    delta_rows = jnp.sum(
        grad_att.astype(jnp.float32) * att_heads.astype(jnp.float32), axis=-1
    ).T
    soft_weights = jnp.where(allowed[None], jnp.exp(scores - log_total[:, :, None]), 0.0)
    grad_value = jnp.einsum(
        "hqk,qhd->khd",
        soft_weights.astype(jnp.bfloat16),
        grad_att,
        preferred_element_type=jnp.float32,
    ).reshape(span, part)
    grad_probs = jnp.einsum(
        "qhd,khd->hqk", grad_att, value_heads, preferred_element_type=jnp.float32
    )
    grad_scores = (soft_weights * (grad_probs - delta_rows[:, :, None])).astype(jnp.bfloat16)
    grad_query = (
        jnp.einsum(
            "hqk,khd->qhd", grad_scores, key_heads, preferred_element_type=jnp.float32
        ).reshape(span, part)
        * attn_scale
    )
    grad_key = (
        jnp.einsum(
            "hqk,qhd->khd", grad_scores, query_heads, preferred_element_type=jnp.float32
        ).reshape(span, part)
        * attn_scale
    )
    grad_proj = jnp.concatenate([grad_query, grad_key, grad_value], axis=1).astype(jnp.bfloat16)
    down_grad, grad_proj = lax.optimization_barrier((down_grad, grad_proj))
    down_grad = down_grad.astype(jnp.float32)
    grad_norm_one = summed(
        back_product(grad_proj, qkv_part).astype(jnp.bfloat16), "ctx", ctx_count
    )
    normed_one, inverse_one = norm_parts(resid_in)
    input_grad = grad_mid + norm_back(grad_norm_one, normed_one, inverse_one, gains[0])

    outw_rows = summed(
        outer_sum(att_part, mid_span).astype(jnp.bfloat16), "dp", dp_count
    ).astype(jnp.bfloat16)
    qkv_rows = summed(
        outer_sum(normed_in, grad_proj).astype(jnp.bfloat16), "dp", dp_count
    ).astype(jnp.bfloat16)
    outw_grad = lax.ppermute(
        outw_rows,
        both,
        [
            (d * ctx_count + c, c * dp_count + d)
            for d in range(dp_count)
            for c in range(ctx_count)
        ],
    ).astype(jnp.float32)
    returned = lax.all_to_all(
        jnp.concatenate([qkv_rows, up_rows], axis=1).reshape(ctx_count, own_rows, -1),
        "ctx",
        0,
        0,
        tiled=True,
    ).astype(jnp.float32)
    qkv_grad = (
        returned[:, :, : 3 * part]
        .reshape(ctx_count, own_rows, 3, part)
        .transpose(1, 2, 0, 3)
        .reshape(own_rows, 3 * width)
    )
    up_grad = (
        returned[:, :, 3 * part :]
        .reshape(ctx_count, own_rows, dp_count, own_hidden)
        .transpose(1, 2, 0, 3)
        .reshape(own_rows, hidden * ctx_count)
    )

    def placed(sums):
        return lax.dynamic_update_slice_in_dim(
            jnp.zeros((width,), jnp.float32), sums, here * part, 0
        )

    feature_sums = jnp.stack(
        [
            jnp.sum(grad_norm_one * normed_one, axis=0),
            jnp.sum(grad_norm_two * normed_two, axis=0),
            jnp.sum(grad_norm_one, axis=0),
            jnp.sum(grad_norm_two, axis=0),
            placed(jnp.sum(grad_query, axis=0)),
            placed(jnp.sum(grad_value, axis=0)),
            jnp.sum(grad_mid, axis=0),
            jnp.sum(grad_top, axis=0),
        ]
    )
    hidden_sums = lax.dynamic_update_slice_in_dim(
        jnp.zeros((dp_count, ctx_count, own_hidden), jnp.float32),
        jnp.sum(grad_pre, axis=0).reshape(dp_count, 1, own_hidden),
        here,
        1,
    ).reshape(dp_count * ctx_count, own_hidden)
    packed = jnp.concatenate(
        [
            feature_sums.reshape(8, -1, own_feats).transpose(1, 0, 2).reshape(-1, 8 * own_feats),
            hidden_sums,
        ],
        axis=1,
    )
    owned = summed(packed, both, dp_count * ctx_count)[0]
    rows = owned[: 8 * own_feats].reshape(8, own_feats)
    return (
        block_out,
        input_grad,
        qkv_grad,
        outw_grad,
        up_grad,
        down_grad,
        rows[0:2],
        rows[2:4],
        rows[4:8],
        owned[8 * own_feats :],
    )


def solution(mesh):
    return jax.shard_map(
        shards,
        mesh=mesh,
        in_specs=(
            P(("dp", "ctx"), None),
            P(("dp", "ctx"), None),
            P("dp", None),
            P("dp", None),
            P(("dp", "ctx"), None),
            P(("dp", "ctx"), None),
            P(("dp", "ctx"), None),
            P(("dp", "ctx"), None),
            P(None, ("dp", "ctx")),
            P(None, ("dp", "ctx")),
            P(None, ("dp", "ctx")),
            P(("dp", "ctx")),
        ),
        out_specs=(
            P(("dp", "ctx"), None),
            P(("dp", "ctx"), None),
            P(("dp", "ctx"), None),
            P(("dp", "ctx"), None),
            P(("dp", "ctx"), None),
            P(("dp", "ctx"), None),
            P(None, ("dp", "ctx")),
            P(None, ("dp", "ctx")),
            P(None, ("dp", "ctx")),
            P(("dp", "ctx")),
        ),
        check_vma=False,
    )
```
